1024 devices in a mesh: cell: 64 (over y, x, core), mem: 16 (over z).
Axes of the slice: x: 4, y: 8, z: 16, core: 2. Of those that a mesh axis runs over, the one named last changes fastest.
Arguments:
- state: bfloat16 [128, 1048576], P('mem', 'cell'), may hold values from -6 to 6
- obs_value: float32 [131072], P('cell'), may hold values from -6 to 6
- obs_error: float32 [131072], P('cell'), may hold values from 0.25 to 1
- obs_cell: int32 [131072], P('cell'), may hold values from 0 to 1023
- obs_count: int32 [1024], P('cell'), may hold values from 32 to 128, as said below
- obs_noise: int32 [131072], P('cell'), may hold values from 0 to 511
- noise_table: float32 [128, 512], P('mem'), may hold values from -6 to 6
Outputs:
- analysis: bfloat16 [128, 1048576], P('mem', 'cell')
The draws below stay inside these ranges and needn't reach their ends.
Inputs may be any that keep to these rules, and one draw needn't show every extreme that they name: `obs_count`: some tile has all 128 slots live in every draw.
All inputs are finite; a program needn't handle non-finite values.
Results may differ from the reference program's by a relative error of at most 0.0062.
Values may be sent and summed in bfloat16 or wider, within the bound.
No kernel may reach another device: no remote copies, remote signals or barrier semaphores. Data moves between devices by JAX's collectives and lax.ppermute only.
A program may use at most 32 MiB of HBM per device.

```python
import math
import jax
import jax.numpy as jnp
from jax import lax

MEMBERS = 128
C_TILE = 1024
OBS_CAP = 128
NOISE = 512
LOCALIZE = 1024
NC = 1048576
NO = 131072


def draw_obs_count(key, part):
    tile_count = NO // OBS_CAP
    first, second = jax.random.split(jax.random.fold_in(key, 7))
    counts = jax.random.randint(first, (tile_count,), OBS_CAP // 4, OBS_CAP + 1)
    full_tile = jax.random.randint(second, (), 0, tile_count)
    return counts.at[full_tile].set(OBS_CAP).astype(jnp.int32)


def plant(array, stream_key, smallest, top_value):
    dims = array.shape
    index_at = [jax.random.randint(jax.random.fold_in(stream_key, axis), (), 0, dims[axis]) for axis in range(len(dims))]
    array = array.at[tuple(index_at)].set(smallest)
    longest = dims.index(max(dims))
    index_at[longest] = (index_at[longest] + 1) % dims[longest]
    return array.at[tuple(index_at)].set(top_value)


def level_of(own_key, extent, shards, least, top_value):
    factor_of, own = 1.0, jax.random.fold_in(own_key, 6)
    for dim, shards_of in shards:
        heights = jnp.exp(jax.random.uniform(jax.random.fold_in(own, dim), (shards_of,), jnp.float32, least / len(shards), top_value / len(shards)))
        factor_of = factor_of * jnp.repeat(heights, extent[dim] // shards_of).reshape([-1 if axis == dim else 1 for axis in range(len(extent))])
    return factor_of


def gaussian(key, dims, width, most, cuts=(), kind=jnp.bfloat16):
    gain = level_of(key, dims, cuts, -0.22, 0.18) if cuts else 1.0
    array = jax.random.normal(key, dims, jnp.float32) * width * gain
    return jnp.minimum(jnp.maximum(array, -most), most).astype(kind)


def setup_inputs(seed: int = 0) -> dict:
    key_list = jax.random.split(jax.random.key(seed), 8)
    return {
        "state": gaussian(key_list[0], (MEMBERS, NC), 1.0, 6.0, ((0, 16), (1, 64))),
        "obs_value": gaussian(key_list[1], (NO,), 1.0, 6.0, ((0, 64),), jnp.float32),
        "obs_error": jnp.clip(jnp.exp(math.log(1.0) - 1.3862944 * jax.random.uniform(key_list[2], (NO,), jnp.float32) ** level_of(key_list[2], (NO,), ((0, 64),), -0.2, 0.2)), 0.25, 1.0),
        "obs_cell": plant(jax.random.randint(key_list[3], (NO,), 0, C_TILE), jax.random.fold_in(key_list[3], 1), 0, C_TILE - 1).astype(jnp.int32),
        "obs_count": draw_obs_count(jax.random.fold_in(key_list[7], 71), 0),
        "obs_noise": plant(jax.random.randint(key_list[5], (NO,), 0, NOISE), jax.random.fold_in(key_list[5], 1), 0, NOISE - 1).astype(jnp.int32),
        "noise_table": gaussian(key_list[6], (MEMBERS, NOISE), 1.0, 6.0, ((0, 16),), jnp.float32),
    }


def reference(state, obs_value, obs_error, obs_cell, obs_count, obs_noise, noise_table):
    tile_count = NC // C_TILE
    state_f32 = state.astype(jnp.float32)
    ens_mean = lax.optimization_barrier(jnp.sum(state_f32, axis=0)) / MEMBERS
    anomaly = (state_f32 - ens_mean).astype(jnp.bfloat16)
    slot_ids = jnp.arange(NO, dtype=jnp.int32)
    tile_of = slot_ids // OBS_CAP
    grid_cell = (tile_of * C_TILE + obs_cell).astype(jnp.int32)
    live_mask = (slot_ids % OBS_CAP < obs_count[tile_of]).astype(jnp.float32)
    at_obs = state_f32[:, grid_cell]
    mean_at = ens_mean[grid_cell]
    spread = (lax.optimization_barrier(jnp.sum(at_obs * at_obs, axis=0)) - MEMBERS * mean_at * mean_at) / (MEMBERS - 1)
    perturb = noise_table[:, obs_noise]
    weight_obs = 1.0 / (spread + obs_error)
    innovation = ((obs_value + jnp.sqrt(obs_error) * perturb - at_obs) * weight_obs * live_mask).astype(jnp.bfloat16)
    obs_anomaly = anomaly[:, grid_cell] * live_mask.astype(jnp.bfloat16)
    position = grid_cell.astype(jnp.float32)
    pad_anom = jnp.pad(obs_anomaly.reshape(MEMBERS, tile_count, OBS_CAP), ((0, 0), (1, 1), (0, 0)))
    pad_innov = jnp.pad(innovation.reshape(MEMBERS, tile_count, OBS_CAP), ((0, 0), (1, 1), (0, 0)))
    pad_pos = jnp.pad(position.reshape(tile_count, OBS_CAP), ((1, 1), (0, 0)))

    def per_tile(tile_index):
        win_anom = lax.dynamic_slice_in_dim(pad_anom, tile_index, 3, 1).reshape(MEMBERS, 3 * OBS_CAP)
        win_innov = lax.dynamic_slice_in_dim(pad_innov, tile_index, 3, 1).reshape(MEMBERS, 3 * OBS_CAP)
        win_pos = lax.dynamic_slice_in_dim(pad_pos, tile_index, 3, 0).reshape(3 * OBS_CAP)
        start = (tile_index * C_TILE).astype(jnp.int32)
        tile_anom = lax.dynamic_slice_in_dim(anomaly, start, C_TILE, 1)
        tile_state = lax.dynamic_slice_in_dim(state_f32, start, C_TILE, 1)
        covariance = lax.dot_general(tile_anom, win_anom, (((0,), (0,)), ((), ())), preferred_element_type=jnp.float32) / (MEMBERS - 1)
        cell_pos = (start + jnp.arange(C_TILE, dtype=jnp.int32)).astype(jnp.float32)
        ratio = jnp.abs(cell_pos[:, None] - win_pos[None, :]) / LOCALIZE
        inner = 1.0 - ratio * ratio
        tapering = jnp.where(ratio < 1.0, inner * inner, 0.0)
        gain_mat = (tapering * covariance).astype(jnp.bfloat16)
        increment = lax.dot_general(win_innov, gain_mat, (((1,), (1,)), ((), ())), preferred_element_type=jnp.float32)
        return (tile_state + increment).astype(jnp.bfloat16)
    result = lax.map(per_tile, jnp.arange(tile_count, dtype=jnp.int32))
    return jnp.transpose(result, (1, 0, 2)).reshape(MEMBERS, NC)
```

```python
import jax
import jax.numpy as jnp
from jax import lax
from jax.experimental import pallas as pl
from jax.experimental.pallas import tpu as pltpu
from jax.sharding import PartitionSpec as P

MEMBERS = 128
C_TILE = 1024
OBS_CAP = 128
NOISE = 512
LOCALIZE = 1024
LANES = 128
CHUNK = 256
POS_BASE = 32
F32 = jnp.float32
BF16 = jnp.bfloat16


def pack_kernel(state_ref, noise_ref, pick_ref, out_ref):
    tiles = out_ref.shape[0]
    mem_dev = state_ref.shape[0]
    table = [noise_ref[:, k * LANES : (k + 1) * LANES] for k in range(NOISE // LANES)]
    for t in range(tiles):
        out_ref[t, :, 0:C_TILE] = state_ref[:, t * C_TILE : (t + 1) * C_TILE]
        pick = jnp.broadcast_to(pick_ref[t : t + 1, :], (mem_dev, OBS_CAP))
        lane, block = pick % LANES, pick // LANES
        chosen = jnp.zeros((mem_dev, OBS_CAP), F32)
        for k, part in enumerate(table):
            here = jnp.take_along_axis(part, lane, axis=1)
            chosen = jnp.where(block == k, here, chosen)
        out_ref[t, :, C_TILE : C_TILE + OBS_CAP] = chosen.astype(BF16)


def pack(state, noise_table, picks):
    mem_dev = state.shape[0]
    tiles = picks.shape[0]
    return pl.pallas_call(
        pack_kernel,
        out_shape=jax.ShapeDtypeStruct((tiles, mem_dev, C_TILE + OBS_CAP), BF16),
        name="pack",
    )(state, noise_table, picks)


def obs_kernel(which_ref, count_ref, tile_ref, value_ref, error_ref, cell_ref, send_ref, anom_ref):
    me = which_ref[0]
    value = value_ref[pl.ds(me, 1), :]
    error = error_ref[pl.ds(me, 1), :]
    cell = cell_ref[pl.ds(me, 1), :]
    live = (lax.broadcasted_iota(jnp.int32, (1, OBS_CAP), 1) < count_ref[me]).astype(F32)
    state = tile_ref[:, 0:C_TILE]
    onehot = (lax.broadcasted_iota(jnp.int32, (C_TILE, OBS_CAP), 0) == cell).astype(F32).astype(BF16)
    at_obs = jnp.dot(state, onehot, preferred_element_type=F32)
    perturb = tile_ref[:, C_TILE : C_TILE + OBS_CAP].astype(F32)
    mean_at = jnp.sum(at_obs, axis=0, keepdims=True) / MEMBERS
    spread = (jnp.sum(at_obs * at_obs, axis=0, keepdims=True) - MEMBERS * mean_at * mean_at) / (
        MEMBERS - 1
    )
    weight = live / (spread + error)
    innovation = (value + jnp.sqrt(error) * perturb - at_obs) * weight
    send_ref[0:MEMBERS, :] = ((at_obs - mean_at) * live).astype(BF16)
    send_ref[MEMBERS : 2 * MEMBERS, :] = innovation.astype(BF16)
    row = lax.broadcasted_iota(jnp.int32, (16, OBS_CAP), 0)
    digits = jnp.where(row == 0, cell // POS_BASE, cell % POS_BASE)
    send_ref[2 * MEMBERS : 2 * MEMBERS + 16, :] = digits.astype(F32).astype(BF16)
    state_f32 = state.astype(F32)
    mean = jnp.sum(state_f32, axis=0, keepdims=True) / MEMBERS
    anom_ref[...] = (state_f32 - mean).astype(BF16)


def obs_stage(which, counts, tile, value, error, cell):
    smem = pl.BlockSpec(memory_space=pltpu.SMEM)
    vmem = pl.BlockSpec(memory_space=pltpu.VMEM)
    return pl.pallas_call(
        obs_kernel,
        in_specs=[smem, smem, vmem, vmem, vmem, vmem],
        out_shape=(
            jax.ShapeDtypeStruct((2 * MEMBERS + 16, OBS_CAP), BF16),
            jax.ShapeDtypeStruct((MEMBERS, C_TILE), BF16),
        ),
        name="obs",
    )(which, counts, tile, value, error, cell)


def increment_of(anom, sent_ref, shift):
    digits = sent_ref[2 * MEMBERS : 2 * MEMBERS + 16, :].astype(F32)
    position = digits[0:1, :] * POS_BASE + digits[1:2, :] + shift
    position = jnp.transpose(jnp.broadcast_to(position, (OBS_CAP, OBS_CAP)))
    covariance = lax.dot_general(
        sent_ref[0:MEMBERS, :], anom, (((0,), (0,)), ((), ())), preferred_element_type=F32
    )
    width = anom.shape[1]
    away = lax.broadcasted_iota(jnp.int32, (OBS_CAP, width), 1).astype(F32) - jnp.concatenate(
        [position] * (width // OBS_CAP), axis=1
    )
    inner = jnp.maximum(1.0 - (away * away) * (1.0 / (LOCALIZE * LOCALIZE)), 0.0)
    gain = (inner * inner * (covariance * (1.0 / (MEMBERS - 1)))).astype(BF16)
    return jnp.dot(sent_ref[MEMBERS : 2 * MEMBERS, :], gain, preferred_element_type=F32)


def own_kernel(tile_ref, anom_ref, sent_ref, out_ref):
    for start in range(0, C_TILE, CHUNK):
        cut = slice(start, start + CHUNK)
        part = increment_of(anom_ref[:, cut], sent_ref, -start)
        out_ref[:, cut] = tile_ref[:, cut].astype(F32) + part


def side_kernel(so_far_ref, anom_ref, low_ref, high_ref, out_ref):
    for start in range(0, C_TILE, CHUNK):
        cut = slice(start, start + CHUNK)
        anom = anom_ref[:, cut]
        total = so_far_ref[:, cut]
        total = total + increment_of(anom, low_ref, -C_TILE - start)
        total = total + increment_of(anom, high_ref, C_TILE - start)
        out_ref[:, cut] = total.astype(BF16)


def body(state, obs_value, obs_error, obs_cell, obs_count, obs_noise, noise_table):
    mem_dev, cell_count = state.shape
    tiles = cell_count // C_TILE
    rows = lambda a: a.reshape(tiles, OBS_CAP)
    packed = pack(state, noise_table, rows(obs_noise))
    tile = lax.all_to_all(packed, "mem", split_axis=0, concat_axis=0, tiled=True)
    tile = tile.reshape(MEMBERS, C_TILE + OBS_CAP)
    which = lax.axis_index("mem").reshape(1)
    sent, anom = obs_stage(which, obs_count, tile, rows(obs_value), rows(obs_error), rows(obs_cell))
    both = ("cell", "mem")
    total = lax.axis_size("cell") * lax.axis_size("mem")
    low = lax.ppermute(sent, both, [(i, i + 1) for i in range(total - 1)])
    high = lax.ppermute(sent, both, [(i + 1, i) for i in range(total - 1)])
    so_far = pl.pallas_call(
        own_kernel, out_shape=jax.ShapeDtypeStruct((MEMBERS, C_TILE), F32), name="own"
    )(tile, anom, sent)
    analysis = pl.pallas_call(
        side_kernel, out_shape=jax.ShapeDtypeStruct((MEMBERS, C_TILE), BF16), name="side"
    )(so_far, anom, low, high)
    returned = lax.all_to_all(
        analysis.reshape(tiles, mem_dev, C_TILE), "mem", split_axis=0, concat_axis=0, tiled=True
    )
    return jnp.transpose(returned, (1, 0, 2)).reshape(mem_dev, cell_count)


def solution(mesh):
    placed = (
        P("mem", "cell"),
        P("cell"),
        P("cell"),
        P("cell"),
        P("cell"),
        P("cell"),
        P("mem", None),
    )
    return jax.shard_map(
        body, mesh=mesh, in_specs=placed, out_specs=P("mem", "cell"), check_vma=False
    )
```

```python
import jax
import jax.numpy as jnp
from jax import lax
from jax.experimental import pallas as pl
from jax.experimental.pallas import tpu as pltpu
from jax.sharding import PartitionSpec as P

MEMBERS = 128
C_TILE = 1024
OBS_CAP = 128
NOISE = 512
LOCALIZE = 1024
LANES = 128
CHUNK = 256
POS_BASE = 32
F32 = jnp.float32
BF16 = jnp.bfloat16


def pack_kernel(state_ref, noise_ref, pick_ref, out_ref):
    tiles = out_ref.shape[0]
    mem_dev = state_ref.shape[0]
    table = [noise_ref[:, k * LANES : (k + 1) * LANES] for k in range(NOISE // LANES)]
    for t in range(tiles):
        out_ref[t, :, 0:C_TILE] = state_ref[:, t * C_TILE : (t + 1) * C_TILE]
        pick = jnp.broadcast_to(pick_ref[t : t + 1, :], (mem_dev, OBS_CAP))
        lane, block = pick % LANES, pick // LANES
        chosen = jnp.zeros((mem_dev, OBS_CAP), F32)
        for k, part in enumerate(table):
            here = jnp.take_along_axis(part, lane, axis=1)
            chosen = jnp.where(block == k, here, chosen)
        out_ref[t, :, C_TILE : C_TILE + OBS_CAP] = chosen.astype(BF16)


def pack(state, noise_table, picks):
    mem_dev = state.shape[0]
    tiles = picks.shape[0]
    return pl.pallas_call(
        pack_kernel,
        out_shape=pltpu.VMEM((tiles, mem_dev, C_TILE + OBS_CAP), BF16),
        name="pack",
    )(state, noise_table, picks)


def obs_kernel(which_ref, count_ref, tile_ref, value_ref, error_ref, cell_ref, send_ref, anom_ref):
    me = which_ref[0]
    value = value_ref[pl.ds(me, 1), :]
    error = error_ref[pl.ds(me, 1), :]
    cell = cell_ref[pl.ds(me, 1), :]
    live = (lax.broadcasted_iota(jnp.int32, (1, OBS_CAP), 1) < count_ref[me]).astype(F32)
    state = tile_ref[:, 0:C_TILE]
    onehot = (lax.broadcasted_iota(jnp.int32, (C_TILE, OBS_CAP), 0) == cell).astype(F32).astype(BF16)
    at_obs = jnp.dot(state, onehot, preferred_element_type=F32)
    perturb = tile_ref[:, C_TILE : C_TILE + OBS_CAP].astype(F32)
    mean_at = jnp.sum(at_obs, axis=0, keepdims=True) / MEMBERS
    spread = (jnp.sum(at_obs * at_obs, axis=0, keepdims=True) - MEMBERS * mean_at * mean_at) / (
        MEMBERS - 1
    )
    weight = live / (spread + error)
    innovation = (value + jnp.sqrt(error) * perturb - at_obs) * weight
    send_ref[0:MEMBERS, :] = ((at_obs - mean_at) * live).astype(BF16)
    send_ref[MEMBERS : 2 * MEMBERS, :] = innovation.astype(BF16)
    row = lax.broadcasted_iota(jnp.int32, (16, OBS_CAP), 0)
    digits = jnp.where(row == 0, cell // POS_BASE, cell % POS_BASE)
    send_ref[2 * MEMBERS : 2 * MEMBERS + 16, :] = digits.astype(F32).astype(BF16)
    state_f32 = state.astype(F32)
    mean = jnp.sum(state_f32, axis=0, keepdims=True) / MEMBERS
    anom_ref[...] = (state_f32 - mean).astype(BF16)


def obs_stage(which, counts, tile, value, error, cell):
    smem = pl.BlockSpec(memory_space=pltpu.SMEM)
    vmem = pl.BlockSpec(memory_space=pltpu.VMEM)
    tile = pltpu.with_memory_space_constraint(tile, pltpu.VMEM)
    return pl.pallas_call(
        obs_kernel,
        in_specs=[smem, smem, vmem, vmem, vmem, vmem],
        out_shape=(
            pltpu.VMEM((2 * MEMBERS + 16, OBS_CAP), BF16),
            pltpu.VMEM((MEMBERS, C_TILE), BF16),
        ),
        name="obs",
    )(which, counts, tile, value, error, cell)


def increment_of(anom, sent_ref, shift):
    digits = sent_ref[2 * MEMBERS : 2 * MEMBERS + 16, :].astype(F32)
    position = digits[0:1, :] * POS_BASE + digits[1:2, :] + shift
    position = jnp.transpose(jnp.broadcast_to(position, (OBS_CAP, OBS_CAP)))
    covariance = lax.dot_general(
        sent_ref[0:MEMBERS, :], anom, (((0,), (0,)), ((), ())), preferred_element_type=F32
    )
    width = anom.shape[1]
    away = lax.broadcasted_iota(jnp.int32, (OBS_CAP, width), 1).astype(F32) - jnp.concatenate(
        [position] * (width // OBS_CAP), axis=1
    )
    inner = jnp.maximum(1.0 - (away * away) * (1.0 / (LOCALIZE * LOCALIZE)), 0.0)
    gain = (inner * inner * (covariance * (1.0 / (MEMBERS - 1)))).astype(BF16)
    return jnp.dot(sent_ref[MEMBERS : 2 * MEMBERS, :], gain, preferred_element_type=F32)


def own_kernel(tile_ref, anom_ref, sent_ref, out_ref):
    for start in range(0, C_TILE, CHUNK):
        cut = slice(start, start + CHUNK)
        part = increment_of(anom_ref[:, cut], sent_ref, -start)
        out_ref[:, cut] = tile_ref[:, cut].astype(F32) + part


def side_kernel(so_far_ref, anom_ref, low_ref, high_ref, out_ref):
    for start in range(0, C_TILE, CHUNK):
        cut = slice(start, start + CHUNK)
        anom = anom_ref[:, cut]
        total = so_far_ref[:, cut]
        total = total + increment_of(anom, low_ref, -C_TILE - start)
        total = total + increment_of(anom, high_ref, C_TILE - start)
        out_ref[:, cut] = total.astype(BF16)


def body(state, obs_value, obs_error, obs_cell, obs_count, obs_noise, noise_table):
    mem_dev, cell_count = state.shape
    tiles = cell_count // C_TILE
    rows = lambda a: a.reshape(tiles, OBS_CAP)
    packed = pack(state, noise_table, rows(obs_noise))
    tile = lax.all_to_all(packed, "mem", split_axis=0, concat_axis=0, tiled=True)
    tile = tile.reshape(MEMBERS, C_TILE + OBS_CAP)
    which = lax.axis_index("mem").reshape(1)
    sent, anom = obs_stage(which, obs_count, tile, rows(obs_value), rows(obs_error), rows(obs_cell))
    both = ("cell", "mem")
    total = lax.axis_size("cell") * lax.axis_size("mem")
    low = lax.ppermute(sent, both, [(i, i + 1) for i in range(total - 1)])
    high = lax.ppermute(sent, both, [(i + 1, i) for i in range(total - 1)])
    v = lambda a: pltpu.with_memory_space_constraint(a, pltpu.VMEM)
    so_far = pl.pallas_call(
        own_kernel, out_shape=pltpu.VMEM((MEMBERS, C_TILE), F32), name="own"
    )(v(tile), v(anom), v(sent))
    analysis = pl.pallas_call(
        side_kernel, out_shape=pltpu.VMEM((MEMBERS, C_TILE), BF16), name="side"
    )(v(so_far), v(anom), v(low), v(high))
    returned = lax.all_to_all(
        analysis.reshape(tiles, mem_dev, C_TILE), "mem", split_axis=0, concat_axis=0, tiled=True
    )
    return jnp.transpose(returned, (1, 0, 2)).reshape(mem_dev, cell_count)


def solution(mesh):
    placed = (
        P("mem", "cell"),
        P("cell"),
        P("cell"),
        P("cell"),
        P("cell"),
        P("cell"),
        P("mem", None),
    )
    return jax.shard_map(
        body, mesh=mesh, in_specs=placed, out_specs=P("mem", "cell"), check_vma=False
    )
```

```python
import jax
import jax.numpy as jnp
from jax import lax
from jax.experimental import pallas as pl
from jax.experimental.pallas import tpu as pltpu
from jax.sharding import PartitionSpec as P

MEMBERS = 128
C_TILE = 1024
OBS_CAP = 128
NOISE = 512
LOCALIZE = 1024
LANES = 128
CHUNK = 256
POS_BASE = 32
SENT_ROWS = 2 * MEMBERS + 16
F32 = jnp.float32
BF16 = jnp.bfloat16
ANY = pl.BlockSpec(memory_space=pl.ANY)
SMEM = pl.BlockSpec(memory_space=pltpu.SMEM)
VMEM = pl.BlockSpec(memory_space=pltpu.VMEM)


def here(x):
    return pltpu.with_memory_space_constraint(x, pltpu.VMEM)


def pack_kernel(state_ref, noise_ref, pick_ref, out_ref, noise, pick, chosen, small, large, back):
    tiles, mem_dev, _ = out_ref.shape
    needed = [
        pltpu.make_async_copy(noise_ref, noise, small.at[0]),
        pltpu.make_async_copy(pick_ref, pick, small.at[1]),
    ]
    for copy in needed:
        copy.start()
    moved = [
        pltpu.make_async_copy(
            state_ref.at[:, t * C_TILE : (t + 1) * C_TILE],
            out_ref.at[t, :, 0:C_TILE],
            large.at[t],
        )
        for t in range(tiles)
    ]
    for copy in moved:
        copy.start()
    for copy in needed:
        copy.wait()
    table = [noise[:, k * LANES : (k + 1) * LANES] for k in range(NOISE // LANES)]
    for t in range(tiles):
        index = jnp.broadcast_to(pick[t : t + 1, :], (mem_dev, OBS_CAP))
        lane, block = index % LANES, index // LANES
        value = jnp.take_along_axis(table[0], lane, axis=1)
        for k in range(1, len(table)):
            value = jnp.where(block == k, jnp.take_along_axis(table[k], lane, axis=1), value)
        chosen[t] = value.astype(BF16)
    last = pltpu.make_async_copy(chosen, out_ref.at[:, :, C_TILE : C_TILE + OBS_CAP], back)
    last.start()
    for copy in moved:
        copy.wait()
    last.wait()


def pack(state, noise_table, picks):
    mem_dev = state.shape[0]
    tiles = picks.shape[0]
    return pl.pallas_call(
        pack_kernel,
        in_specs=[ANY, ANY, ANY],
        out_specs=ANY,
        out_shape=jax.ShapeDtypeStruct((tiles, mem_dev, C_TILE + OBS_CAP), BF16),
        scratch_shapes=[
            pltpu.VMEM((mem_dev, NOISE), F32),
            pltpu.VMEM((tiles, OBS_CAP), jnp.int32),
            pltpu.VMEM((tiles, mem_dev, OBS_CAP), BF16),
            pltpu.SemaphoreType.DMA((2,)),
            pltpu.SemaphoreType.DMA((tiles,)),
            pltpu.SemaphoreType.DMA,
        ],
        name="pack",
    )(state, noise_table, picks)


def ready_kernel(which_ref, count_ref, value_ref, error_ref, cell_ref, hot_ref, row_ref, pos_ref):
    me = which_ref[0]
    error = error_ref[pl.ds(me, 1), :]
    cell = cell_ref[pl.ds(me, 1), :]
    live = lax.broadcasted_iota(jnp.int32, (1, OBS_CAP), 1) < count_ref[me]
    row_ref[0:1, :] = value_ref[pl.ds(me, 1), :]
    row_ref[1:2, :] = error
    row_ref[2:3, :] = jnp.sqrt(error)
    row_ref[3:4, :] = live.astype(F32)
    row_ref[4:8, :] = jnp.zeros((4, OBS_CAP), F32)
    cells = lax.broadcasted_iota(jnp.int32, (C_TILE, OBS_CAP), 0)
    hot_ref[...] = (cells == cell).astype(F32).astype(BF16)
    row = lax.broadcasted_iota(jnp.int32, (16, OBS_CAP), 0)
    digits = jnp.where(row == 0, cell // POS_BASE, cell % POS_BASE)
    pos_ref[...] = jnp.where(row == 2, me % 2, digits).astype(F32).astype(BF16)


def obs_kernel(tile_ref, hot_ref, row_ref, pos_ref, send_ref):
    value, error, root, live = (row_ref[k : k + 1, :] for k in range(4))
    at_obs = jnp.dot(tile_ref[:, 0:C_TILE], hot_ref[...], preferred_element_type=F32)
    perturb = tile_ref[:, C_TILE : C_TILE + OBS_CAP].astype(F32)
    mean_at = jnp.sum(at_obs, axis=0, keepdims=True) / MEMBERS
    spread = (jnp.sum(at_obs * at_obs, axis=0, keepdims=True) - MEMBERS * mean_at * mean_at) / (
        MEMBERS - 1
    )
    weight = live / (spread + error)
    innovation = (value + root * perturb - at_obs) * weight
    send_ref[0:MEMBERS, :] = ((at_obs - mean_at) * live).astype(BF16)
    send_ref[MEMBERS : 2 * MEMBERS, :] = innovation.astype(BF16)
    send_ref[2 * MEMBERS : SENT_ROWS, :] = pos_ref[...]


def slots_of(sent_ref, side):
    digits = sent_ref[2 * MEMBERS : SENT_ROWS, :].astype(F32)
    shift = (2.0 * digits[2:3, :] - 1.0) * float(side * C_TILE)
    position = digits[0:1, :] * POS_BASE + digits[1:2, :] + shift
    position = jnp.transpose(jnp.broadcast_to(position, (OBS_CAP, OBS_CAP)))
    wide = jnp.concatenate([position] * (CHUNK // OBS_CAP), axis=1)
    return sent_ref[0:MEMBERS, :], sent_ref[MEMBERS : 2 * MEMBERS, :], wide


def increment_of(anom, slots, start):
    obs_anom, innovation, position = slots
    covariance = lax.dot_general(
        obs_anom, anom, (((0,), (0,)), ((), ())), preferred_element_type=F32
    )
    cells = lax.broadcasted_iota(jnp.int32, (OBS_CAP, CHUNK), 1).astype(F32) + float(start)
    away = cells - position
    inner = jnp.maximum(1.0 - (away * away) * (1.0 / (LOCALIZE * LOCALIZE)), 0.0)
    gain = (inner * inner * (covariance * (1.0 / (MEMBERS - 1)))).astype(BF16)
    return jnp.dot(innovation, gain, preferred_element_type=F32)


def own_kernel(tile_ref, sent_ref, anom_ref, out_ref):
    slots = slots_of(sent_ref, 0)
    for start in range(0, C_TILE, CHUNK):
        cut = slice(start, start + CHUNK)
        state = tile_ref[:, cut].astype(F32)
        anom = (state - jnp.sum(state, axis=0, keepdims=True) / MEMBERS).astype(BF16)
        anom_ref[:, cut] = anom
        out_ref[:, cut] = state + increment_of(anom, slots, start)


def side_kernel(so_far_ref, anom_ref, near_ref, far_ref, out_ref):
    near = slots_of(near_ref, 1)
    far = slots_of(far_ref, -1)
    for start in range(0, C_TILE, CHUNK):
        cut = slice(start, start + CHUNK)
        anom = anom_ref[:, cut]
        total = so_far_ref[:, cut]
        total = total + increment_of(anom, near, start) + increment_of(anom, far, start)
        out_ref[:, cut] = total.astype(BF16)


def swapped(x, first):
    axes = ("cell", "mem")
    count = lax.axis_size("cell") * lax.axis_size("mem")
    pairs = [(i, i + 1) for i in range(first, count - 1, 2)]
    return lax.ppermute(x, axes, pairs + [(j, i) for i, j in pairs])


def body(state, obs_value, obs_error, obs_cell, obs_count, obs_noise, noise_table):
    mem_dev, cell_count = state.shape
    tiles = cell_count // C_TILE
    rows = lambda a: a.reshape(tiles, OBS_CAP)
    which = lax.axis_index("mem").reshape(1)
    packed = pack(state, noise_table, rows(obs_noise))
    tile = lax.all_to_all(packed, "mem", split_axis=0, concat_axis=0, tiled=True)
    tile = tile.reshape(MEMBERS, C_TILE + OBS_CAP)
    hot, numbers, digits = pl.pallas_call(
        ready_kernel,
        in_specs=[SMEM, SMEM, VMEM, VMEM, VMEM],
        out_shape=(
            pltpu.VMEM((C_TILE, OBS_CAP), BF16),
            pltpu.VMEM((8, OBS_CAP), F32),
            pltpu.VMEM((16, OBS_CAP), BF16),
        ),
        name="ready",
    )(which, obs_count, rows(obs_value), rows(obs_error), rows(obs_cell))
    sent = pl.pallas_call(
        obs_kernel, out_shape=pltpu.VMEM((SENT_ROWS, OBS_CAP), BF16), name="obs"
    )(here(tile), here(hot), here(numbers), here(digits))
    near = swapped(sent, 0)
    far = swapped(sent, 1)
    anom, so_far = pl.pallas_call(
        own_kernel,
        out_shape=(pltpu.VMEM((MEMBERS, C_TILE), BF16), pltpu.VMEM((MEMBERS, C_TILE), F32)),
        name="own",
    )(here(tile), here(sent))
    analysis = pl.pallas_call(
        side_kernel, out_shape=pltpu.VMEM((MEMBERS, C_TILE), BF16), name="side"
    )(here(so_far), here(anom), here(near), here(far))
    returned = lax.all_to_all(
        analysis.reshape(tiles, mem_dev, C_TILE), "mem", split_axis=0, concat_axis=0, tiled=True
    )
    return jnp.transpose(returned, (1, 0, 2)).reshape(mem_dev, cell_count)


def solution(mesh):
    placed = (
        P("mem", "cell"),
        P("cell"),
        P("cell"),
        P("cell"),
        P("cell"),
        P("cell"),
        P("mem", None),
    )
    return jax.shard_map(
        body, mesh=mesh, in_specs=placed, out_specs=P("mem", "cell"), check_vma=False
    )
```

```python
import jax
import jax.numpy as jnp
from jax import lax
from jax.experimental import pallas as pl
from jax.experimental.pallas import tpu as pltpu
from jax.sharding import PartitionSpec as P

MEMBERS = 128
C_TILE = 1024
OBS_CAP = 128
NOISE = 512
LOCALIZE = 1024
LANES = 128
CHUNK = 256
POS_BASE = 32
SENT_ROWS = 2 * MEMBERS + 16
F32 = jnp.float32
BF16 = jnp.bfloat16
ANY = pl.BlockSpec(memory_space=pl.ANY)
SMEM = pl.BlockSpec(memory_space=pltpu.SMEM)
VMEM = pl.BlockSpec(memory_space=pltpu.VMEM)


def here(x):
    return pltpu.with_memory_space_constraint(x, pltpu.VMEM)


def place_of(tile, flipped, tiles):
    return tile + flipped * (tiles - 1 - 2 * tile)


def spot_of(device, tiles):
    flipped = lax.rem(lax.div(device, tiles), 2)
    return place_of(lax.rem(device, tiles), flipped, tiles), flipped


def prepare_kernel(
    where_ref, count_ref, state_ref, noise_ref, pick_ref, value_ref, error_ref, cell_ref,
    out_ref, hot_ref, row_ref, pos_ref, sem,
):
    tiles, mem_dev, _ = out_ref.shape
    me, flipped = spot_of(where_ref[0], tiles)
    places = [place_of(t, flipped, tiles) for t in range(tiles)]
    moved = [
        pltpu.make_async_copy(
            state_ref.at[:, t * C_TILE : (t + 1) * C_TILE],
            out_ref.at[places[t], :, 0:C_TILE],
            sem.at[t],
        )
        for t in range(tiles)
    ]
    for copy in moved:
        copy.start()
    table = [noise_ref[:, k * LANES : (k + 1) * LANES] for k in range(NOISE // LANES)]
    for t in range(tiles):
        index = jnp.broadcast_to(pick_ref[t : t + 1, :], (mem_dev, OBS_CAP))
        lane, block = index % LANES, index // LANES
        value = jnp.take_along_axis(table[0], lane, axis=1)
        for k in range(1, len(table)):
            value = jnp.where(block == k, jnp.take_along_axis(table[k], lane, axis=1), value)
        out_ref[places[t], :, C_TILE : C_TILE + OBS_CAP] = value.astype(BF16)
    error = error_ref[pl.ds(me, 1), :]
    cell = cell_ref[pl.ds(me, 1), :]
    live = lax.broadcasted_iota(jnp.int32, (1, OBS_CAP), 1) < count_ref[me]
    row_ref[0:1, :] = value_ref[pl.ds(me, 1), :]
    row_ref[1:2, :] = error
    row_ref[2:3, :] = jnp.sqrt(error)
    row_ref[3:4, :] = live.astype(F32)
    row_ref[4:8, :] = jnp.zeros((4, OBS_CAP), F32)
    cells = lax.broadcasted_iota(jnp.int32, (C_TILE, OBS_CAP), 0)
    hot_ref[...] = (cells == cell).astype(F32).astype(BF16)
    row = lax.broadcasted_iota(jnp.int32, (16, OBS_CAP), 0)
    digits = jnp.where(row == 0, cell // POS_BASE, cell % POS_BASE)
    pos_ref[...] = jnp.where(row == 2, lax.rem(me, 2), digits).astype(F32).astype(BF16)
    for copy in moved:
        copy.wait()


def restore_kernel(where_ref, back_ref, out_ref, sem):
    tiles = back_ref.shape[0]
    _, flipped = spot_of(where_ref[0], tiles)
    moved = [
        pltpu.make_async_copy(
            back_ref.at[place_of(t, flipped, tiles)],
            out_ref.at[:, t * C_TILE : (t + 1) * C_TILE],
            sem.at[t],
        )
        for t in range(tiles)
    ]
    for copy in moved:
        copy.start()
    for copy in moved:
        copy.wait()


def obs_kernel(tile_ref, hot_ref, row_ref, pos_ref, send_ref):
    value, error, root, live = (row_ref[k : k + 1, :] for k in range(4))
    at_obs = jnp.dot(tile_ref[:, 0:C_TILE], hot_ref[...], preferred_element_type=F32)
    perturb = tile_ref[:, C_TILE : C_TILE + OBS_CAP].astype(F32)
    mean_at = jnp.sum(at_obs, axis=0, keepdims=True) / MEMBERS
    spread = (jnp.sum(at_obs * at_obs, axis=0, keepdims=True) - MEMBERS * mean_at * mean_at) / (
        MEMBERS - 1
    )
    weight = live / (spread + error)
    innovation = (value + root * perturb - at_obs) * weight
    send_ref[0:MEMBERS, :] = ((at_obs - mean_at) * live).astype(BF16)
    send_ref[MEMBERS : 2 * MEMBERS, :] = innovation.astype(BF16)
    send_ref[2 * MEMBERS : SENT_ROWS, :] = pos_ref[...]


def slots_of(sent_ref, side):
    digits = sent_ref[2 * MEMBERS : SENT_ROWS, :].astype(F32)
    shift = (2.0 * digits[2:3, :] - 1.0) * float(side * C_TILE)
    position = digits[0:1, :] * POS_BASE + digits[1:2, :] + shift
    position = jnp.transpose(jnp.broadcast_to(position, (OBS_CAP, OBS_CAP)))
    wide = jnp.concatenate([position] * (CHUNK // OBS_CAP), axis=1)
    return sent_ref[0:MEMBERS, :], sent_ref[MEMBERS : 2 * MEMBERS, :], wide


def increment_of(anom, slots, start):
    obs_anom, innovation, position = slots
    covariance = lax.dot_general(
        obs_anom, anom, (((0,), (0,)), ((), ())), preferred_element_type=F32
    )
    cells = lax.broadcasted_iota(jnp.int32, (OBS_CAP, CHUNK), 1).astype(F32) + float(start)
    away = cells - position
    inner = jnp.maximum(1.0 - (away * away) * (1.0 / (LOCALIZE * LOCALIZE)), 0.0)
    gain = (inner * inner * (covariance * (1.0 / (MEMBERS - 1)))).astype(BF16)
    return jnp.dot(innovation, gain, preferred_element_type=F32)


def own_kernel(tile_ref, sent_ref, anom_ref, out_ref):
    slots = slots_of(sent_ref, 0)
    for start in range(0, C_TILE, CHUNK):
        cut = slice(start, start + CHUNK)
        state = tile_ref[:, cut].astype(F32)
        anom = (state - jnp.sum(state, axis=0, keepdims=True) / MEMBERS).astype(BF16)
        anom_ref[:, cut] = anom
        out_ref[:, cut] = state + increment_of(anom, slots, start)


def side_kernel(so_far_ref, anom_ref, near_ref, far_ref, out_ref):
    near = slots_of(near_ref, 1)
    far = slots_of(far_ref, -1)
    for start in range(0, C_TILE, CHUNK):
        cut = slice(start, start + CHUNK)
        anom = anom_ref[:, cut]
        total = so_far_ref[:, cut]
        total = total + increment_of(anom, near, start) + increment_of(anom, far, start)
        out_ref[:, cut] = total.astype(BF16)


def swapped(x, first):
    shards, tiles = lax.axis_size("cell"), lax.axis_size("mem")
    line = [
        shard * tiles + place_of(tile, shard % 2, tiles)
        for shard in range(shards)
        for tile in range(tiles)
    ]
    pairs = [(line[i], line[i + 1]) for i in range(first, len(line) - 1, 2)]
    return lax.ppermute(x, ("cell", "mem"), pairs + [(j, i) for i, j in pairs])


def body(state, obs_value, obs_error, obs_cell, obs_count, obs_noise, noise_table):
    mem_dev, cell_count = state.shape
    tiles = cell_count // C_TILE
    rows = lambda a: a.reshape(tiles, OBS_CAP)
    where = lax.axis_index(("cell", "mem")).reshape(1)
    packed, hot, numbers, digits = pl.pallas_call(
        prepare_kernel,
        in_specs=[SMEM, SMEM, ANY, VMEM, VMEM, VMEM, VMEM, VMEM],
        out_shape=(
            pltpu.VMEM((tiles, mem_dev, C_TILE + OBS_CAP), BF16),
            pltpu.VMEM((C_TILE, OBS_CAP), BF16),
            pltpu.VMEM((8, OBS_CAP), F32),
            pltpu.VMEM((16, OBS_CAP), BF16),
        ),
        scratch_shapes=[pltpu.SemaphoreType.DMA((tiles,))],
        name="prepare",
    )(
        where, obs_count, state, noise_table,
        rows(obs_noise), rows(obs_value), rows(obs_error), rows(obs_cell),
    )
    tile = lax.all_to_all(packed, "mem", split_axis=0, concat_axis=0, tiled=True)
    tile = tile.reshape(MEMBERS, C_TILE + OBS_CAP)
    sent = pl.pallas_call(
        obs_kernel, out_shape=pltpu.VMEM((SENT_ROWS, OBS_CAP), BF16), name="obs"
    )(here(tile), here(hot), here(numbers), here(digits))
    near = swapped(sent, 0)
    far = swapped(sent, 1)
    anom, so_far = pl.pallas_call(
        own_kernel,
        out_shape=(pltpu.VMEM((MEMBERS, C_TILE), BF16), pltpu.VMEM((MEMBERS, C_TILE), F32)),
        name="own",
    )(here(tile), here(sent))
    analysis = pl.pallas_call(
        side_kernel, out_shape=pltpu.VMEM((MEMBERS, C_TILE), BF16), name="side"
    )(here(so_far), here(anom), here(near), here(far))
    returned = lax.all_to_all(
        analysis.reshape(tiles, mem_dev, C_TILE), "mem", split_axis=0, concat_axis=0, tiled=True
    )
    return pl.pallas_call(
        restore_kernel,
        in_specs=[SMEM, VMEM],
        out_specs=ANY,
        out_shape=jax.ShapeDtypeStruct((mem_dev, cell_count), BF16),
        scratch_shapes=[pltpu.SemaphoreType.DMA((tiles,))],
        name="restore",
    )(where, here(returned))


def solution(mesh):
    placed = (
        P("mem", "cell"),
        P("cell"),
        P("cell"),
        P("cell"),
        P("cell"),
        P("cell"),
        P("mem", None),
    )
    return jax.shard_map(
        body, mesh=mesh, in_specs=placed, out_specs=P("mem", "cell"), check_vma=False
    )
```

```python
import jax
import jax.numpy as jnp
from jax import lax
from jax.experimental import pallas as pl
from jax.experimental.pallas import tpu as pltpu
from jax.sharding import PartitionSpec as P


MEMBERS = 128
C_TILE = 1024
OBS_CAP = 128
NOISE = 512
LOCALIZE = 1024
LANES = 128
CHUNK = 256
POS_BASE = 32
SENT_ROWS = 2 * MEMBERS + 16
F32 = jnp.float32
BF16 = jnp.bfloat16
ANY = pl.BlockSpec(memory_space=pl.ANY)


def here(x):
    return pltpu.with_memory_space_constraint(x, pltpu.VMEM)


def place_of(tile, flipped, tiles):
    return tile + flipped * (tiles - 1 - 2 * tile)


def spot_of(device, tiles):
    flipped = lax.rem(lax.div(device, tiles), 2)
    return place_of(lax.rem(device, tiles), flipped, tiles), flipped


def prepare_kernel(
    count_hbm, state_hbm, noise_hbm, pick_hbm, value_hbm, error_hbm, cell_hbm,
    out_ref, hot_ref, row_ref, pos_ref,
    count_ref, noise_ref, pick_ref, value_ref, error_ref, cell_ref, sem, small,
):
    tiles, mem_dev, _ = out_ref.shape
    me, flipped = spot_of(lax.axis_index(("cell", "mem")), tiles)
    places = [place_of(t, flipped, tiles) for t in range(tiles)]
    inputs = (
        (noise_hbm, noise_ref),
        (pick_hbm, pick_ref),
        (cell_hbm, cell_ref),
        (value_hbm, value_ref),
        (error_hbm, error_ref),
        (count_hbm, count_ref),
    )
    read = [pltpu.make_async_copy(a, b, small.at[k]) for k, (a, b) in enumerate(inputs)]
    for copy in read:
        copy.start()
    moved = [
        pltpu.make_async_copy(
            state_hbm.at[:, t * C_TILE : (t + 1) * C_TILE],
            out_ref.at[places[t], :, 0:C_TILE],
            sem.at[t],
        )
        for t in range(tiles)
    ]
    for copy in moved:
        copy.start()
    for copy in read[:2]:
        copy.wait()
    table = [noise_ref[:, k * LANES : (k + 1) * LANES] for k in range(NOISE // LANES)]
    for t in range(tiles):
        index = jnp.broadcast_to(pick_ref[t : t + 1, :], (mem_dev, OBS_CAP))
        lane, block = index % LANES, index // LANES
        value = jnp.take_along_axis(table[0], lane, axis=1)
        for k in range(1, len(table)):
            value = jnp.where(block == k, jnp.take_along_axis(table[k], lane, axis=1), value)
        out_ref[places[t], :, C_TILE : C_TILE + OBS_CAP] = value.astype(BF16)
    for copy in read[2:]:
        copy.wait()
    error = error_ref[pl.ds(me, 1), :]
    cell = cell_ref[pl.ds(me, 1), :]
    live = lax.broadcasted_iota(jnp.int32, (1, OBS_CAP), 1) < count_ref[me]
    row_ref[0:1, :] = value_ref[pl.ds(me, 1), :]
    row_ref[1:2, :] = error
    row_ref[2:3, :] = jnp.sqrt(error)
    row_ref[3:4, :] = live.astype(F32)
    row_ref[4:8, :] = jnp.zeros((4, OBS_CAP), F32)
    cells = lax.broadcasted_iota(jnp.int32, (C_TILE, OBS_CAP), 0)
    hot_ref[...] = (cells == cell).astype(F32).astype(BF16)
    row = lax.broadcasted_iota(jnp.int32, (16, OBS_CAP), 0)
    digits = jnp.where(row == 0, cell // POS_BASE, cell % POS_BASE)
    pos_ref[...] = jnp.where(row == 2, lax.rem(me, 2), digits).astype(F32).astype(BF16)
    for copy in moved:
        copy.wait()


def restore_kernel(back_ref, out_ref, sem):
    tiles = back_ref.shape[0]
    _, flipped = spot_of(lax.axis_index(("cell", "mem")), tiles)
    moved = [
        pltpu.make_async_copy(
            back_ref.at[place_of(t, flipped, tiles)],
            out_ref.at[:, t * C_TILE : (t + 1) * C_TILE],
            sem.at[t],
        )
        for t in range(tiles)
    ]
    for copy in moved:
        copy.start()
    for copy in moved:
        copy.wait()


def obs_kernel(tile_ref, hot_ref, row_ref, pos_ref, send_ref):
    value, error, root, live = (row_ref[k : k + 1, :] for k in range(4))
    at_obs = jnp.dot(tile_ref[:, 0:C_TILE], hot_ref[...], preferred_element_type=F32)
    perturb = tile_ref[:, C_TILE : C_TILE + OBS_CAP].astype(F32)
    mean_at = jnp.sum(at_obs, axis=0, keepdims=True) / MEMBERS
    spread = (jnp.sum(at_obs * at_obs, axis=0, keepdims=True) - MEMBERS * mean_at * mean_at) / (
        MEMBERS - 1
    )
    weight = live / (spread + error)
    innovation = (value + root * perturb - at_obs) * weight
    send_ref[0:MEMBERS, :] = ((at_obs - mean_at) * live).astype(BF16)
    send_ref[MEMBERS : 2 * MEMBERS, :] = innovation.astype(BF16)
    send_ref[2 * MEMBERS : SENT_ROWS, :] = pos_ref[...]


def slots_of(sent_ref, side):
    digits = sent_ref[2 * MEMBERS : SENT_ROWS, :].astype(F32)
    shift = (2.0 * digits[2:3, :] - 1.0) * float(side * C_TILE)
    position = digits[0:1, :] * POS_BASE + digits[1:2, :] + shift
    position = jnp.transpose(jnp.broadcast_to(position, (OBS_CAP, OBS_CAP)))
    wide = jnp.concatenate([position] * (CHUNK // OBS_CAP), axis=1)
    return sent_ref[0:MEMBERS, :], sent_ref[MEMBERS : 2 * MEMBERS, :], wide


def increment_of(anom, slots, start):
    obs_anom, innovation, position = slots
    covariance = lax.dot_general(
        obs_anom, anom, (((0,), (0,)), ((), ())), preferred_element_type=F32
    )
    cells = lax.broadcasted_iota(jnp.int32, (OBS_CAP, CHUNK), 1).astype(F32) + float(start)
    away = cells - position
    inner = jnp.maximum(1.0 - (away * away) * (1.0 / (LOCALIZE * LOCALIZE)), 0.0)
    gain = (inner * inner * (covariance * (1.0 / (MEMBERS - 1)))).astype(BF16)
    return jnp.dot(innovation, gain, preferred_element_type=F32)


def own_kernel(tile_ref, sent_ref, anom_ref, out_ref):
    slots = slots_of(sent_ref, 0)
    for start in range(0, C_TILE, CHUNK):
        cut = slice(start, start + CHUNK)
        state = tile_ref[:, cut].astype(F32)
        anom = (state - jnp.sum(state, axis=0, keepdims=True) / MEMBERS).astype(BF16)
        anom_ref[:, cut] = anom
        out_ref[:, cut] = state + increment_of(anom, slots, start)


def side_kernel(so_far_ref, anom_ref, near_ref, far_ref, out_ref):
    near = slots_of(near_ref, 1)
    far = slots_of(far_ref, -1)
    for start in range(0, C_TILE, CHUNK):
        cut = slice(start, start + CHUNK)
        anom = anom_ref[:, cut]
        total = so_far_ref[:, cut]
        total = total + increment_of(anom, near, start) + increment_of(anom, far, start)
        out_ref[:, cut] = total.astype(BF16)


def swapped(x, first):
    shards, tiles = lax.axis_size("cell"), lax.axis_size("mem")
    line = [
        shard * tiles + place_of(tile, shard % 2, tiles)
        for shard in range(shards)
        for tile in range(tiles)
    ]
    pairs = [(line[i], line[i + 1]) for i in range(first, len(line) - 1, 2)]
    return lax.ppermute(x, ("cell", "mem"), pairs + [(j, i) for i, j in pairs])


def body(state, obs_value, obs_error, obs_cell, obs_count, obs_noise, noise_table):
    mem_dev, cell_count = state.shape
    tiles = cell_count // C_TILE
    rows = lambda a: a.reshape(tiles, OBS_CAP)
    packed, hot, numbers, digits = pl.pallas_call(
        prepare_kernel,
        in_specs=[ANY] * 7,
        out_shape=(
            pltpu.VMEM((tiles, mem_dev, C_TILE + OBS_CAP), BF16),
            pltpu.VMEM((C_TILE, OBS_CAP), BF16),
            pltpu.VMEM((8, OBS_CAP), F32),
            pltpu.VMEM((16, OBS_CAP), BF16),
        ),
        scratch_shapes=[
            pltpu.SMEM((tiles,), jnp.int32),
            pltpu.VMEM((mem_dev, NOISE), F32),
            pltpu.VMEM((tiles, OBS_CAP), jnp.int32),
            pltpu.VMEM((tiles, OBS_CAP), F32),
            pltpu.VMEM((tiles, OBS_CAP), F32),
            pltpu.VMEM((tiles, OBS_CAP), jnp.int32),
            pltpu.SemaphoreType.DMA((tiles,)),
            pltpu.SemaphoreType.DMA((6,)),
        ],
        name="prepare",
    )(
        obs_count, state, noise_table,
        rows(obs_noise), rows(obs_value), rows(obs_error), rows(obs_cell),
    )
    tile = lax.all_to_all(packed, "mem", split_axis=0, concat_axis=0, tiled=True)
    tile = tile.reshape(MEMBERS, C_TILE + OBS_CAP)
    sent = pl.pallas_call(
        obs_kernel, out_shape=pltpu.VMEM((SENT_ROWS, OBS_CAP), BF16), name="obs"
    )(here(tile), here(hot), here(numbers), here(digits))
    far = swapped(sent, 1)
    near = swapped(sent, 0)
    anom, so_far = pl.pallas_call(
        own_kernel,
        out_shape=(pltpu.VMEM((MEMBERS, C_TILE), BF16), pltpu.VMEM((MEMBERS, C_TILE), F32)),
        name="own",
    )(here(tile), here(sent))
    analysis = pl.pallas_call(
        side_kernel, out_shape=pltpu.VMEM((MEMBERS, C_TILE), BF16), name="side"
    )(here(so_far), here(anom), here(near), here(far))
    returned = lax.all_to_all(
        analysis.reshape(tiles, mem_dev, C_TILE), "mem", split_axis=0, concat_axis=0, tiled=True
    )
    return pl.pallas_call(
        restore_kernel,
        out_specs=ANY,
        out_shape=jax.ShapeDtypeStruct((mem_dev, cell_count), BF16),
        scratch_shapes=[pltpu.SemaphoreType.DMA((tiles,))],
        name="restore",
    )(here(returned))


def solution(mesh):
    placed = (
        P("mem", "cell"),
        P("cell"),
        P("cell"),
        P("cell"),
        P("cell"),
        P("cell"),
        P("mem", None),
    )
    return jax.shard_map(
        body, mesh=mesh, in_specs=placed, out_specs=P("mem", "cell"), check_vma=False
    )
```

```python
import functools

import jax
import jax.numpy as jnp
from jax import lax
from jax.experimental import pallas as pl
from jax.experimental.pallas import tpu as pltpu
from jax.sharding import PartitionSpec as P


MEMBERS = 128
C_TILE = 1024
OBS_CAP = 128
NOISE = 512
LOCALIZE = 1024
LANES = 128
CHUNK = 256
POS_BASE = 32
STRIDE = 1
SENT_ROWS = 2 * MEMBERS + 16
F32 = jnp.float32
BF16 = jnp.bfloat16
ANY = pl.BlockSpec(memory_space=pl.ANY)


def here(x):
    return pltpu.with_memory_space_constraint(x, pltpu.VMEM)


def order_of(tiles):
    return [(STRIDE * k) % tiles for k in range(tiles)]


def place_of(tile, flipped, tiles):
    return tile + flipped * (tiles - 1 - 2 * tile)


def tile_of(device, tiles):
    return place_of(lax.rem(device, tiles), lax.rem(lax.div(device, tiles), 2), tiles)


def prepare_kernel(
    count_hbm, state_hbm, noise_hbm, pick_hbm, value_hbm, error_hbm, cell_hbm,
    out_ref, hot_ref, row_ref, pos_ref,
    count_ref, noise_ref, pick_ref, value_ref, error_ref, cell_ref, sem, small,
):
    tiles, mem_dev, _ = out_ref.shape
    me = tile_of(lax.axis_index(("cell", "mem")), tiles)
    order = order_of(tiles)
    slots = [order.index(t) for t in range(tiles)]
    inputs = (
        (noise_hbm, noise_ref),
        (pick_hbm, pick_ref),
        (cell_hbm, cell_ref),
        (value_hbm, value_ref),
        (error_hbm, error_ref),
        (count_hbm, count_ref),
    )
    read = [pltpu.make_async_copy(a, b, small.at[k]) for k, (a, b) in enumerate(inputs)]
    for copy in read:
        copy.start()
    moved = [
        pltpu.make_async_copy(
            state_hbm.at[:, t * C_TILE : (t + 1) * C_TILE],
            out_ref.at[slots[t], :, 0:C_TILE],
            sem.at[t],
        )
        for t in range(tiles)
    ]
    for copy in moved:
        copy.start()
    for copy in read[:2]:
        copy.wait()
    table = [noise_ref[:, k * LANES : (k + 1) * LANES] for k in range(NOISE // LANES)]
    for t in range(tiles):
        index = jnp.broadcast_to(pick_ref[t : t + 1, :], (mem_dev, OBS_CAP))
        lane, block = index % LANES, index // LANES
        value = jnp.take_along_axis(table[0], lane, axis=1)
        for k in range(1, len(table)):
            value = jnp.where(block == k, jnp.take_along_axis(table[k], lane, axis=1), value)
        out_ref[slots[t], :, C_TILE : C_TILE + OBS_CAP] = value.astype(BF16)
    for copy in read[2:]:
        copy.wait()
    error = error_ref[pl.ds(me, 1), :]
    cell = cell_ref[pl.ds(me, 1), :]
    live = lax.broadcasted_iota(jnp.int32, (1, OBS_CAP), 1) < count_ref[me]
    row_ref[0:1, :] = value_ref[pl.ds(me, 1), :]
    row_ref[1:2, :] = error
    row_ref[2:3, :] = jnp.sqrt(error)
    row_ref[3:4, :] = live.astype(F32)
    edge = jnp.logical_or(me == 0, me == tiles - 1)
    row_ref[4:5, :] = jnp.full((1, OBS_CAP), edge.astype(jnp.int32)).astype(F32)
    row_ref[5:8, :] = jnp.zeros((3, OBS_CAP), F32)
    cells = lax.broadcasted_iota(jnp.int32, (C_TILE, OBS_CAP), 0)
    hot_ref[...] = (cells == cell).astype(F32).astype(BF16)
    row = lax.broadcasted_iota(jnp.int32, (16, OBS_CAP), 0)
    digits = jnp.where(row == 0, cell // POS_BASE, cell % POS_BASE)
    pos_ref[...] = jnp.where(row == 2, lax.rem(me, 2), digits).astype(F32).astype(BF16)
    for copy in moved:
        copy.wait()


def restore_kernel(back_ref, out_ref, sem):
    moved = [
        pltpu.make_async_copy(
            back_ref.at[k], out_ref.at[:, t * C_TILE : (t + 1) * C_TILE], sem.at[k]
        )
        for k, t in enumerate(order_of(back_ref.shape[0]))
    ]
    for copy in moved:
        copy.start()
    for copy in moved:
        copy.wait()


def restored(returned):
    tiles, mem_dev, cells = returned.shape
    return pl.pallas_call(
        restore_kernel,
        out_specs=ANY,
        out_shape=jax.ShapeDtypeStruct((mem_dev, tiles * cells), BF16),
        scratch_shapes=[pltpu.SemaphoreType.DMA((tiles,))],
        name="restore",
    )(here(returned))


def in_other_order(x, tiles):
    order = order_of(tiles)
    size = MEMBERS // tiles
    source = [order.index(tiles - 1 - t) for t in order]
    return jnp.concatenate([x[k * size : (k + 1) * size, :] for k in source], axis=0)


def obs_kernel(tile_ref, hot_ref, row_ref, pos_ref, near_ref, far_ref, *, tiles):
    value, error, root, live, edge = (row_ref[k : k + 1, :] for k in range(5))
    at_obs = jnp.dot(tile_ref[:, 0:C_TILE], hot_ref[...], preferred_element_type=F32)
    perturb = tile_ref[:, C_TILE : C_TILE + OBS_CAP].astype(F32)
    mean_at = jnp.sum(at_obs, axis=0, keepdims=True) / MEMBERS
    spread = (jnp.sum(at_obs * at_obs, axis=0, keepdims=True) - MEMBERS * mean_at * mean_at) / (
        MEMBERS - 1
    )
    weight = live / (spread + error)
    obs_anom = (at_obs - mean_at) * live
    innovation = (value + root * perturb - at_obs) * weight
    for k, rows in enumerate((obs_anom, innovation)):
        cut = slice(k * MEMBERS, (k + 1) * MEMBERS)
        near_ref[cut, :] = rows.astype(BF16)
        far_ref[cut, :] = jnp.where(edge > 0.0, in_other_order(rows, tiles), rows).astype(BF16)
    near_ref[2 * MEMBERS : SENT_ROWS, :] = pos_ref[...]
    far_ref[2 * MEMBERS : SENT_ROWS, :] = pos_ref[...]


def slots_of(sent_ref, side):
    digits = sent_ref[2 * MEMBERS : SENT_ROWS, :].astype(F32)
    shift = (2.0 * digits[2:3, :] - 1.0) * float(side * C_TILE)
    position = digits[0:1, :] * POS_BASE + digits[1:2, :] + shift
    position = jnp.transpose(jnp.broadcast_to(position, (OBS_CAP, OBS_CAP)))
    wide = jnp.concatenate([position] * (CHUNK // OBS_CAP), axis=1)
    return sent_ref[0:MEMBERS, :], sent_ref[MEMBERS : 2 * MEMBERS, :], wide


def increment_of(anom, slots, start):
    obs_anom, innovation, position = slots
    covariance = lax.dot_general(
        obs_anom, anom, (((0,), (0,)), ((), ())), preferred_element_type=F32
    )
    cells = lax.broadcasted_iota(jnp.int32, (OBS_CAP, CHUNK), 1).astype(F32) + float(start)
    away = cells - position
    inner = jnp.maximum(1.0 - (away * away) * (1.0 / (LOCALIZE * LOCALIZE)), 0.0)
    gain = (inner * inner * (covariance * (1.0 / (MEMBERS - 1)))).astype(BF16)
    return jnp.dot(innovation, gain, preferred_element_type=F32)


def own_kernel(tile_ref, sent_ref, anom_ref, out_ref):
    slots = slots_of(sent_ref, 0)
    for start in range(0, C_TILE, CHUNK):
        cut = slice(start, start + CHUNK)
        state = tile_ref[:, cut].astype(F32)
        anom = (state - jnp.sum(state, axis=0, keepdims=True) / MEMBERS).astype(BF16)
        anom_ref[:, cut] = anom
        out_ref[:, cut] = state + increment_of(anom, slots, start)


def side_kernel(so_far_ref, anom_ref, sent_ref, out_ref, *, side):
    slots = slots_of(sent_ref, side)
    for start in range(0, C_TILE, CHUNK):
        cut = slice(start, start + CHUNK)
        total = so_far_ref[:, cut] + increment_of(anom_ref[:, cut], slots, start)
        out_ref[:, cut] = total.astype(out_ref.dtype)


def beside(so_far, anom, sent, side, dtype):
    return pl.pallas_call(
        functools.partial(side_kernel, side=side), out_shape=pltpu.VMEM((MEMBERS, C_TILE), dtype)
    )(here(so_far), here(anom), here(sent))


def line_of_tiles():
    shards, tiles = lax.axis_size("cell"), lax.axis_size("mem")
    return [
        [shard * tiles + place_of(tile, shard % 2, tiles) for tile in range(tiles)]
        for shard in range(shards)
    ]


def exchanged(x):
    return lax.all_to_all(
        x,
        ("cell", "mem"),
        split_axis=0,
        concat_axis=0,
        axis_index_groups=[[shard[t] for t in order_of(len(shard))] for shard in line_of_tiles()],
        tiled=True,
    )


def swapped(x, first):
    line = sum(line_of_tiles(), [])
    pairs = [(line[i], line[i + 1]) for i in range(first, len(line) - 1, 2)]
    return lax.ppermute(x, ("cell", "mem"), pairs + [(j, i) for i, j in pairs])


def body(state, obs_value, obs_error, obs_cell, obs_count, obs_noise, noise_table):
    mem_dev, cell_count = state.shape
    tiles = cell_count // C_TILE
    rows = lambda a: a.reshape(tiles, OBS_CAP)
    packed, hot, numbers, digits = pl.pallas_call(
        prepare_kernel,
        in_specs=[ANY] * 7,
        out_shape=(
            pltpu.VMEM((tiles, mem_dev, C_TILE + OBS_CAP), BF16),
            pltpu.VMEM((C_TILE, OBS_CAP), BF16),
            pltpu.VMEM((8, OBS_CAP), F32),
            pltpu.VMEM((16, OBS_CAP), BF16),
        ),
        scratch_shapes=[
            pltpu.SMEM((tiles,), jnp.int32),
            pltpu.VMEM((mem_dev, NOISE), F32),
            pltpu.VMEM((tiles, OBS_CAP), jnp.int32),
            pltpu.VMEM((tiles, OBS_CAP), F32),
            pltpu.VMEM((tiles, OBS_CAP), F32),
            pltpu.VMEM((tiles, OBS_CAP), jnp.int32),
            pltpu.SemaphoreType.DMA((tiles,)),
            pltpu.SemaphoreType.DMA((6,)),
        ],
        name="prepare",
    )(
        obs_count, state, noise_table,
        rows(obs_noise), rows(obs_value), rows(obs_error), rows(obs_cell),
    )
    tile = exchanged(packed)
    tile = tile.reshape(MEMBERS, C_TILE + OBS_CAP)
    sent, sent_far = pl.pallas_call(
        functools.partial(obs_kernel, tiles=tiles),
        out_shape=(pltpu.VMEM((SENT_ROWS, OBS_CAP), BF16),) * 2,
        name="obs",
    )(here(tile), here(hot), here(numbers), here(digits))
    far = swapped(sent_far, 1)
    near = swapped(sent, 0)
    anom, so_far = pl.pallas_call(
        own_kernel,
        out_shape=(
            pltpu.VMEM((MEMBERS, C_TILE), BF16),
            pltpu.VMEM((MEMBERS, C_TILE), F32),
        ),
        name="own",
    )(here(tile), here(sent))
    so_far = beside(so_far, anom, far, -1, F32)
    analysis = beside(so_far, anom, near, 1, BF16)
    returned = exchanged(analysis.reshape(tiles, mem_dev, C_TILE))
    if order_of(tiles) != list(range(tiles)):
        return restored(returned)
    return jnp.transpose(returned, (1, 0, 2)).reshape(mem_dev, cell_count)


def solution(mesh):
    placed = (
        P("mem", "cell"),
        P("cell"),
        P("cell"),
        P("cell"),
        P("cell"),
        P("cell"),
        P("mem", None),
    )
    return jax.shard_map(
        body, mesh=mesh, in_specs=placed, out_specs=P("mem", "cell"), check_vma=False
    )
```

```python
import functools

import jax
import jax.numpy as jnp
from jax import lax
from jax.experimental import pallas as pl
from jax.experimental.pallas import tpu as pltpu
from jax.sharding import PartitionSpec as P


MEMBERS = 128
C_TILE = 1024
OBS_CAP = 128
NOISE = 512
LOCALIZE = 1024
LANES = 128
CHUNK = 256
POS_BASE = 32
STRIDE = 1
SENT_ROWS = 2 * MEMBERS + 16
F32 = jnp.float32
BF16 = jnp.bfloat16
ANY = pl.BlockSpec(memory_space=pl.ANY)


def here(x):
    return pltpu.with_memory_space_constraint(x, pltpu.VMEM)


def order_of(tiles):
    return [(STRIDE * k) % tiles for k in range(tiles)]


def place_of(tile, flipped, tiles):
    return tile + flipped * (tiles - 1 - 2 * tile)


def tile_of(device, tiles):
    return place_of(lax.rem(device, tiles), lax.rem(lax.div(device, tiles), 2), tiles)


def prepare_kernel(
    count_hbm, state_hbm, noise_hbm, pick_hbm, value_hbm, error_hbm, cell_hbm,
    out_ref, hot_ref, row_ref, pos_ref,
    count_ref, noise_ref, pick_ref, value_ref, error_ref, cell_ref, sem, small,
):
    tiles, mem_dev, _ = out_ref.shape
    me = tile_of(lax.axis_index(("cell", "mem")), tiles)
    order = order_of(tiles)
    slots = [order.index(t) for t in range(tiles)]
    inputs = (
        (noise_hbm, noise_ref),
        (pick_hbm, pick_ref),
        (cell_hbm, cell_ref),
        (value_hbm, value_ref),
        (error_hbm, error_ref),
        (count_hbm, count_ref),
    )
    read = [pltpu.make_async_copy(a, b, small.at[k]) for k, (a, b) in enumerate(inputs)]
    for copy in read[:2]:
        copy.start()
    moved = [
        pltpu.make_async_copy(
            state_hbm.at[:, t * C_TILE : (t + 1) * C_TILE],
            out_ref.at[slots[t], :, 0:C_TILE],
            sem.at[t],
        )
        for t in range(tiles)
    ]
    for copy in moved + read[2:]:
        copy.start()
    for copy in read[:2]:
        copy.wait()
    table = [noise_ref[:, k * LANES : (k + 1) * LANES] for k in range(NOISE // LANES)]
    for t in range(tiles):
        index = jnp.broadcast_to(pick_ref[t : t + 1, :], (mem_dev, OBS_CAP))
        lane, block = jnp.bitwise_and(index, LANES - 1), lax.shift_right_logical(index, LANES.bit_length() - 1)
        value = jnp.take_along_axis(table[0], lane, axis=1)
        for k in range(1, len(table)):
            value = jnp.where(block == k, jnp.take_along_axis(table[k], lane, axis=1), value)
        out_ref[slots[t], :, C_TILE : C_TILE + OBS_CAP] = value.astype(BF16)
    for copy in read[2:]:
        copy.wait()
    error = error_ref[pl.ds(me, 1), :]
    cell = cell_ref[pl.ds(me, 1), :]
    live = lax.broadcasted_iota(jnp.int32, (1, OBS_CAP), 1) < count_ref[me]
    row_ref[0:1, :] = value_ref[pl.ds(me, 1), :]
    row_ref[1:2, :] = error
    row_ref[2:3, :] = jnp.sqrt(error)
    row_ref[3:4, :] = live.astype(F32)
    edge = jnp.logical_or(me == 0, me == tiles - 1)
    row_ref[4:5, :] = jnp.full((1, OBS_CAP), edge.astype(jnp.int32)).astype(F32)
    odd = lax.rem(me, 2)
    above = cell_ref[pl.ds(me + 1 - 2 * odd, 1), :] + C_TILE * (1 - 2 * odd)
    row_ref[5:6, :] = above.astype(F32)
    row_ref[6:7, :] = cell.astype(F32)
    row_ref[7:8, :] = jnp.zeros((1, OBS_CAP), F32)
    cells = lax.broadcasted_iota(jnp.int32, (C_TILE, OBS_CAP), 0)
    hot_ref[...] = (cells == cell).astype(F32).astype(BF16)
    row = lax.broadcasted_iota(jnp.int32, (16, OBS_CAP), 0)
    digits = jnp.where(row == 0, lax.div(cell, POS_BASE), lax.rem(cell, POS_BASE))
    pos_ref[...] = jnp.where(row == 2, lax.rem(me, 2), digits).astype(F32).astype(BF16)
    for copy in moved:
        copy.wait()


def restore_kernel(back_ref, out_ref, sem):
    moved = [
        pltpu.make_async_copy(
            back_ref.at[k], out_ref.at[:, t * C_TILE : (t + 1) * C_TILE], sem.at[k]
        )
        for k, t in enumerate(order_of(back_ref.shape[0]))
    ]
    for copy in moved:
        copy.start()
    for copy in moved:
        copy.wait()


def restored(returned):
    tiles, mem_dev, cells = returned.shape
    return pl.pallas_call(
        restore_kernel,
        out_specs=ANY,
        out_shape=jax.ShapeDtypeStruct((mem_dev, tiles * cells), BF16),
        scratch_shapes=[pltpu.SemaphoreType.DMA((tiles,))],
        name="restore",
    )(here(returned))


def in_other_order(x, tiles):
    order = order_of(tiles)
    size = MEMBERS // tiles
    source = [order.index(tiles - 1 - t) for t in order]
    return jnp.concatenate([x[k * size : (k + 1) * size, :] for k in source], axis=0)


def obs_kernel(tile_ref, hot_ref, row_ref, pos_ref, near_ref, far_ref, *, tiles):
    value, error, root, live, edge = (row_ref[k : k + 1, :] for k in range(5))
    at_obs = jnp.dot(tile_ref[:, 0:C_TILE], hot_ref[...], preferred_element_type=F32)
    perturb = tile_ref[:, C_TILE : C_TILE + OBS_CAP].astype(F32)
    mean_at = jnp.sum(at_obs, axis=0, keepdims=True) / MEMBERS
    spread = (jnp.sum(at_obs * at_obs, axis=0, keepdims=True) - MEMBERS * mean_at * mean_at) / (
        MEMBERS - 1
    )
    weight = live / (spread + error)
    obs_anom = (at_obs - mean_at) * live
    innovation = (value + root * perturb - at_obs) * weight
    for k, rows in enumerate((obs_anom, innovation)):
        cut = slice(k * MEMBERS, (k + 1) * MEMBERS)
        near_ref[cut, :] = rows.astype(BF16)
        far_ref[cut, :] = jnp.where(edge > 0.0, in_other_order(rows, tiles), rows).astype(BF16)
    far_ref[2 * MEMBERS : SENT_ROWS, :] = pos_ref[...]


def column(row):
    square = jnp.transpose(jnp.broadcast_to(row, (OBS_CAP, OBS_CAP)))
    return jnp.concatenate([square] * (CHUNK // OBS_CAP), axis=1)


def far_position(sent_ref):
    digits = sent_ref[2 * MEMBERS : SENT_ROWS, :].astype(F32)
    shift = (1.0 - 2.0 * digits[2:3, :]) * float(C_TILE)
    return column(digits[0:1, :] * POS_BASE + digits[1:2, :] + shift)


def taper_of(position, start):
    cells = lax.broadcasted_iota(jnp.int32, (OBS_CAP, CHUNK), 1).astype(F32) + float(start)
    away = cells - position
    inner = jnp.maximum(1.0 - (away * away) * (1.0 / (LOCALIZE * LOCALIZE)), 0.0)
    return inner * inner * (1.0 / (MEMBERS - 1))


def increment_of(anom, sent_ref, taper):
    covariance = lax.dot_general(
        sent_ref[0:MEMBERS, :], anom, (((0,), (0,)), ((), ())), preferred_element_type=F32
    )
    gain = (taper * covariance).astype(BF16)
    return jnp.dot(sent_ref[MEMBERS : 2 * MEMBERS, :], gain, preferred_element_type=F32)


STRETCHES = [(start, slice(start, start + CHUNK)) for start in range(0, C_TILE, CHUNK)]


def own_kernel(tile_ref, sent_ref, row_ref, anom_ref, out_ref, taper_ref):
    position = column(row_ref[6:7, :])
    for start, cut in STRETCHES:
        state = tile_ref[:, cut].astype(F32)
        anom = (state - jnp.sum(state, axis=0, keepdims=True) / MEMBERS).astype(BF16)
        anom_ref[:, cut] = anom
        out_ref[:, cut] = state + increment_of(anom, sent_ref, taper_of(position, start))
    position = column(row_ref[5:6, :])
    for start, cut in STRETCHES:
        taper_ref[:, cut] = taper_of(position, start)


def far_kernel(so_far_ref, anom_ref, sent_ref, out_ref):
    position = far_position(sent_ref)
    for start, cut in STRETCHES:
        part = increment_of(anom_ref[:, cut], sent_ref, taper_of(position, start))
        out_ref[:, cut] = so_far_ref[:, cut] + part


def near_kernel(so_far_ref, anom_ref, taper_ref, sent_ref, out_ref):
    for _, cut in STRETCHES:
        part = increment_of(anom_ref[:, cut], sent_ref, taper_ref[:, cut])
        out_ref[:, cut] = (so_far_ref[:, cut] + part).astype(BF16)


def line_of_tiles():
    shards, tiles = lax.axis_size("cell"), lax.axis_size("mem")
    return [
        [shard * tiles + place_of(tile, shard % 2, tiles) for tile in range(tiles)]
        for shard in range(shards)
    ]


def exchanged(x):
    return lax.all_to_all(
        x,
        ("cell", "mem"),
        split_axis=0,
        concat_axis=0,
        axis_index_groups=[[shard[t] for t in order_of(len(shard))] for shard in line_of_tiles()],
        tiled=True,
    )


def swapped(x, first):
    line = sum(line_of_tiles(), [])
    pairs = [(line[i], line[i + 1]) for i in range(first, len(line) - 1, 2)]
    return lax.ppermute(x, ("cell", "mem"), pairs + [(j, i) for i, j in pairs])


def body(state, obs_value, obs_error, obs_cell, obs_count, obs_noise, noise_table):
    mem_dev, cell_count = state.shape
    tiles = cell_count // C_TILE
    rows = lambda a: a.reshape(tiles, OBS_CAP)
    packed, hot, numbers, digits = pl.pallas_call(
        prepare_kernel,
        in_specs=[ANY] * 7,
        out_shape=(
            pltpu.VMEM((tiles, mem_dev, C_TILE + OBS_CAP), BF16),
            pltpu.VMEM((C_TILE, OBS_CAP), BF16),
            pltpu.VMEM((8, OBS_CAP), F32),
            pltpu.VMEM((16, OBS_CAP), BF16),
        ),
        scratch_shapes=[
            pltpu.SMEM((tiles,), jnp.int32),
            pltpu.VMEM((mem_dev, NOISE), F32),
            pltpu.VMEM((tiles, OBS_CAP), jnp.int32),
            pltpu.VMEM((tiles, OBS_CAP), F32),
            pltpu.VMEM((tiles, OBS_CAP), F32),
            pltpu.VMEM((tiles, OBS_CAP), jnp.int32),
            pltpu.SemaphoreType.DMA((tiles,)),
            pltpu.SemaphoreType.DMA((6,)),
        ],
        name="prepare",
    )(
        obs_count, state, noise_table,
        rows(obs_noise), rows(obs_value), rows(obs_error), rows(obs_cell),
    )
    tile = exchanged(packed)
    tile = tile.reshape(MEMBERS, C_TILE + OBS_CAP)
    sent, sent_far = pl.pallas_call(
        functools.partial(obs_kernel, tiles=tiles),
        out_shape=(
            pltpu.VMEM((2 * MEMBERS, OBS_CAP), BF16),
            pltpu.VMEM((SENT_ROWS, OBS_CAP), BF16),
        ),
        name="obs",
    )(here(tile), here(hot), here(numbers), here(digits))
    far = swapped(sent_far, 1)
    near = swapped(sent, 0)
    anom, so_far, taper = pl.pallas_call(
        own_kernel,
        out_shape=(
            pltpu.VMEM((MEMBERS, C_TILE), BF16),
            pltpu.VMEM((MEMBERS, C_TILE), F32),
            pltpu.VMEM((OBS_CAP, C_TILE), F32),
        ),
        name="own",
    )(here(tile), here(sent), here(numbers))
    so_far = pl.pallas_call(
        far_kernel, out_shape=pltpu.VMEM((MEMBERS, C_TILE), F32), name="far"
    )(here(so_far), here(anom), here(far))
    analysis = pl.pallas_call(
        near_kernel, out_shape=pltpu.VMEM((MEMBERS, C_TILE), BF16), name="near"
    )(here(so_far), here(anom), here(taper), here(near))
    returned = exchanged(analysis.reshape(tiles, mem_dev, C_TILE))
    if order_of(tiles) != list(range(tiles)):
        return restored(returned)
    return jnp.transpose(returned, (1, 0, 2)).reshape(mem_dev, cell_count)


def solution(mesh):
    placed = (
        P("mem", "cell"),
        P("cell"),
        P("cell"),
        P("cell"),
        P("cell"),
        P("cell"),
        P("mem", None),
    )
    return jax.shard_map(
        body, mesh=mesh, in_specs=placed, out_specs=P("mem", "cell"), check_vma=False
    )
```
